32 devices in a mesh: row: 2 (over y), col: 8 (over z, x), depth: 2 (over core).
Axes of the slice: x: 2, y: 2, z: 4, core: 2. Of those that a mesh axis runs over, the one named last changes fastest.
Arguments:
- a_tiles: bfloat16 [2, 16, 8, 2, 128, 128], P('row', ('col', 'depth')), may hold values from -1.5 to 1.5
- a_cols: int32 [2, 16, 8, 2], P('row', ('col', 'depth')), may hold values from 0 to 15, as said below
- a_count: int32 [2, 16, 8], P('row', ('col', 'depth')), may hold values from 0 to 2, as said below
- b_tiles: bfloat16 [4, 2, 2, 8, 16, 1, 128, 128], P(None, 'row', 'depth', 'col'), may hold values from -1.5 to 1.5
- b_cols: int32 [4, 2, 2, 8, 16, 1], P(None, 'row', 'depth', 'col'), may hold values from 0 to 11, as said below
- b_count: int32 [4, 2, 2, 8, 16], P(None, 'row', 'depth', 'col'), may hold values from 0 to 1, as said below
Outputs:
- product: bfloat16 [2048, 12288], P(('row', 'depth'), 'col')
The draws below stay inside these ranges and needn't reach their ends.
Inputs may be any that keep to these rules, and one draw needn't show every extreme that they name: The entries of a_cols for one row group, inner panel and block row are distinct. `a_count`: some block row holds 2 blocks in every draw. The entries of b_cols for one inner block row are distinct. `b_count`: some inner block row holds 1 block in every draw.
All inputs are finite; a program needn't handle non-finite values.
Results may differ from the reference program's by a relative error of at most 0.001.
Values may be sent and summed in bfloat16 or wider, within the bound.
A program may use at most 128 MiB of HBM per device.

```python
import jax
import jax.numpy as jnp
from jax import lax

TILE = 128
KB = 16
BR = 8
BC = 12
TPR = 2
TPK = 1
SHIFTS = 4
SLOTS = 4
PANELS = 16
ROWS = 2048
COLS = 12288
N_ROW = 2
N_COL = 8
N_DEPTH = 2


def distinct_lists(key, leading, width, needed):
    scores = jax.random.randint(key, leading + (width,), 0, 1 << 20, dtype=jnp.int32) * width + jnp.arange(width, dtype=jnp.int32)
    order_ids = jnp.argsort(scores, axis=-1, stable=True)
    return order_ids[..., :needed].astype(jnp.int32)


def bounded_counts(key, shape_all, most):
    first_key, second_key = jax.random.split(key)
    counts = jax.random.randint(first_key, shape_all, 0, most + 1, dtype=jnp.int32)
    flat_counts = counts.reshape(-1)
    chosen_spot = jax.random.randint(second_key, (), 0, flat_counts.shape[0], dtype=jnp.int32)
    flat_counts = flat_counts.at[chosen_spot].set(most)
    return flat_counts.reshape(shape_all)


def draw_a_cols(key, part):
    return distinct_lists(jax.random.fold_in(key, 11), (N_ROW, PANELS, BR), KB, TPR)


def draw_a_count(key, part):
    return bounded_counts(jax.random.fold_in(key, 12), (N_ROW, PANELS, BR), TPR)


def draw_b_cols(key, part):
    return distinct_lists(jax.random.fold_in(key, 13), (SLOTS, N_ROW, N_DEPTH, N_COL, KB), BC, TPK)


def draw_b_count(key, part):
    return bounded_counts(jax.random.fold_in(key, 14), (SLOTS, N_ROW, N_DEPTH, N_COL, KB), TPK)


def steps_of(own_key, extent, shards, least, high):
    factor_of, own = 1.0, jax.random.fold_in(own_key, 6)
    for axis_at, shards_of in shards:
        draws = jnp.exp(jax.random.uniform(jax.random.fold_in(own, axis_at), (shards_of,), jnp.float32, least / len(shards), high / len(shards)))
        factor_of = factor_of * jnp.repeat(draws, extent[axis_at] // shards_of).reshape([-1 if axis == axis_at else 1 for axis in range(len(extent))])
    return factor_of


def bell_draw(rng, extent, deviation, most, cuts=(), held_as=jnp.bfloat16):
    drawn = deviation * jax.random.normal(rng, extent, jnp.float32)
    if cuts:
        drawn = drawn * steps_of(rng, extent, cuts, -0.22, 0.18)
    return jnp.clip(drawn, -most, most).astype(held_as)


def setup_inputs(seed: int = 0) -> dict:
    key_list = jax.random.split(jax.random.key(seed), 7)
    a_tiles = bell_draw(key_list[0], (N_ROW, PANELS, BR, TPR, TILE, TILE), 0.25, 1.5, ((0, 2), (1, 16)))
    a_cols = draw_a_cols(jax.random.fold_in(key_list[6], 71), 0)
    a_count = draw_a_count(jax.random.fold_in(key_list[6], 71), 0)
    b_tiles = bell_draw(key_list[3], (SLOTS, N_ROW, N_DEPTH, N_COL, KB, TPK, TILE, TILE), 0.25, 1.5, ((1, 2), (2, 2), (3, 8)))
    b_cols = draw_b_cols(jax.random.fold_in(key_list[6], 71), 0)
    b_count = draw_b_count(jax.random.fold_in(key_list[6], 71), 0)
    return dict(a_tiles=a_tiles, a_cols=a_cols, a_count=a_count, b_tiles=b_tiles, b_cols=b_cols, b_count=b_count)


def dense_panel(tiles_b, cols_b, count_b):
    slot_ids = lax.broadcasted_iota(jnp.int32, cols_b.shape, 1)
    valid_slot = slot_ids < count_b[:, None]
    targets = jnp.arange(BC, dtype=jnp.int32)
    placing = jnp.logical_and(cols_b[:, :, None] == targets[None, None, :], valid_slot[:, :, None]).astype(jnp.float32)
    spread = jnp.einsum("kuc,kuab->kacb", placing, tiles_b.astype(jnp.float32), precision=lax.Precision.HIGHEST)
    return spread.astype(jnp.bfloat16).reshape(KB, TILE, BC * TILE)


def panel_product(tiles_a, cols_a, count_a, rows_dense):
    slot_ids = lax.broadcasted_iota(jnp.int32, cols_a.shape, 1)
    valid_slot = slot_ids < count_a[:, None]
    masked = jnp.where(valid_slot[:, :, None, None], tiles_a, jnp.zeros_like(tiles_a))
    chosen = jnp.take(rows_dense, cols_a, axis=0)
    return jnp.einsum("rtab,rtbn->ran", masked.astype(jnp.float32), chosen.astype(jnp.float32), precision=lax.Precision.HIGHEST)


def reference(a_tiles, a_cols, a_count, b_tiles, b_cols, b_count):
    def one_block(flat_index):
        row_group = flat_index // N_COL
        col_group = flat_index % N_COL
        running = jnp.zeros((BR, TILE, BC * TILE), jnp.float32)
        for depth_id in range(N_DEPTH):
            for turn_no in range(SHIFTS):
                panel_no = (row_group + col_group + turn_no) % N_COL
                inner_panel = panel_no * N_DEPTH + depth_id
                slot_no = panel_no // N_ROW
                member = panel_no % N_ROW
                rows_dense = dense_panel(b_tiles[slot_no, member, depth_id, col_group], b_cols[slot_no, member, depth_id, col_group], b_count[slot_no, member, depth_id, col_group])
                running = running + panel_product(a_tiles[row_group, inner_panel], a_cols[row_group, inner_panel], a_count[row_group, inner_panel], rows_dense)
        return running.reshape(BR * TILE, BC * TILE).astype(jnp.bfloat16)

    blocks = lax.map(one_block, jnp.arange(N_ROW * N_COL, dtype=jnp.int32))
    blocks = blocks.reshape(N_ROW, N_COL, BR * TILE, BC * TILE)
    return jnp.transpose(blocks, (0, 2, 1, 3)).reshape(ROWS, COLS)
```

```python
import functools
import math

import jax
import jax.numpy as jnp
from jax import lax
from jax.experimental import pallas as pl
from jax.experimental.pallas import tpu as pltpu
from jax.sharding import PartitionSpec as P

BC = 12
SHIFTS = 4


def for_sending(array):
    return jax.tree.map(lambda a: a.astype(jnp.bfloat16) if a.dtype == jnp.float32 else a, array)


def shifted(value, axis, steps):
    count = lax.axis_size(axis)
    pairs = [(source, (source + steps) % count) for source in range(count)]
    return lax.ppermute(value, axis, pairs)


def dense_panel(tiles_b, cols_b, count_b, width):
    slot_ids = lax.broadcasted_iota(jnp.int32, cols_b.shape, 1)
    valid_slot = slot_ids < count_b[:, None]
    targets = lax.broadcasted_iota(jnp.int32, (1, 1, width), 2)
    placing = jnp.logical_and(cols_b[:, :, None] == targets, valid_slot[:, :, None]).astype(
        jnp.bfloat16
    )
    spread = jnp.einsum("kuc,kuab->kacb", placing, tiles_b, preferred_element_type=jnp.float32)
    inner_blocks = tiles_b.shape[0]
    tile_size = tiles_b.shape[2]
    return spread.astype(jnp.bfloat16).reshape(inner_blocks, tile_size, width * tile_size)


def panel_product(tiles_a, cols_a, count_a, rows_dense):
    block_rows = tiles_a.shape[0]
    per_row = tiles_a.shape[1]
    tile_size = tiles_a.shape[2]
    slot_ids = lax.broadcasted_iota(jnp.int32, cols_a.shape, 1)
    valid_slot = slot_ids < count_a[:, None]
    masked = jnp.where(valid_slot[:, :, None, None], tiles_a, jnp.zeros_like(tiles_a))
    group_rows = math.gcd(block_rows, 4)

    def one_group(pieces):
        tiles_part, cols_part = pieces
        chosen = jnp.take(rows_dense, cols_part, axis=0)
        return jnp.einsum("rtab,rtbn->ran", tiles_part, chosen, preferred_element_type=jnp.float32)

    grouped = lax.map(
        one_group,
        (
            masked.reshape(block_rows // group_rows, group_rows, per_row, tile_size, tile_size),
            cols_a.reshape(block_rows // group_rows, group_rows, per_row),
        ),
    )
    return grouped.reshape(block_rows, tile_size, rows_dense.shape[2])


def roll_slots(stack, offset):
    slot_total = stack[0].shape[0]
    return tuple(
        (
            lax.dynamic_slice_in_dim(
                jnp.concatenate([member, member], 0), offset % slot_total, slot_total, 0
            )
            for member in stack
        )
    )


def select_if(flag, fresh, stale):
    return tuple((jnp.where(flag, new_part, old_part) for new_part, old_part in zip(fresh, stale)))


def local(a_tiles, a_cols, a_count, b_tiles, b_cols, b_count):
    rows_axis = lax.axis_size("row")
    cols_axis = lax.axis_size("col")
    row_group = lax.axis_index("row")
    col_group = lax.axis_index("col")
    tiles_a = a_tiles[0, 0]
    cols_a = a_cols[0, 0]
    count_a = a_count[0, 0]
    tiles_b = b_tiles[:, 0, 0, 0]
    cols_b = b_cols[:, 0, 0, 0]
    count_b = b_count[:, 0, 0, 0]
    for bit_pos in range((rows_axis - 1).bit_length()):
        stride = 1 << bit_pos
        moved = (
            shifted(tiles_a, "col", cols_axis - stride),
            shifted(for_sending(cols_a), "col", cols_axis - stride).astype(cols_a.dtype),
            shifted(for_sending(count_a), "col", cols_axis - stride).astype(count_a.dtype),
        )
        tiles_a, cols_a, count_a = select_if(
            row_group // stride % 2 == 1, moved, (tiles_a, cols_a, count_a)
        )
    for bit_pos in range((cols_axis - 1).bit_length()):
        stride = 1 << bit_pos
        nearby = stride % rows_axis
        if nearby:
            moved = (
                shifted(tiles_b, "row", rows_axis - nearby),
                shifted(for_sending(cols_b), "row", rows_axis - nearby).astype(cols_b.dtype),
                shifted(for_sending(count_b), "row", rows_axis - nearby).astype(count_b.dtype),
            )
        else:
            moved = (tiles_b, cols_b, count_b)
        moved = roll_slots(moved, (row_group + stride) // rows_axis)
        tiles_b, cols_b, count_b = select_if(
            col_group // stride % 2 == 1, moved, (tiles_b, cols_b, count_b)
        )
    tile_size = tiles_a.shape[2]
    running = jnp.zeros((tiles_a.shape[0], tile_size, BC * tile_size), jnp.float32)
    for turn_no in range(SHIFTS):
        current_tiles = tiles_b[0]
        current_cols = cols_b[0]
        current_count = count_b[0]
        rows_dense = dense_panel(current_tiles, current_cols, current_count, BC)
        running = running + panel_product(tiles_a, cols_a, count_a, rows_dense)
        if turn_no + 1 < SHIFTS:
            tiles_a, cols_a, count_a = (
                shifted(tiles_a, "col", cols_axis - 1),
                shifted(for_sending(cols_a), "col", cols_axis - 1).astype(cols_a.dtype),
                shifted(for_sending(count_a), "col", cols_axis - 1).astype(count_a.dtype),
            )
            moved = (
                shifted(tiles_b, "row", rows_axis - 1),
                shifted(for_sending(cols_b), "row", rows_axis - 1).astype(cols_b.dtype),
                shifted(for_sending(count_b), "row", rows_axis - 1).astype(count_b.dtype),
            )
            tiles_b, cols_b, count_b = roll_slots(moved, (row_group + 1) // rows_axis)
    flat_running = running.reshape(-1, running.shape[2])
    summed = lax.psum(flat_running, "depth")
    half_rows = flat_running.shape[0] // lax.axis_size("depth")
    own_rows = lax.dynamic_slice_in_dim(summed, lax.axis_index("depth") * half_rows, half_rows, 0)
    return own_rows.astype(jnp.bfloat16)


REACH = SHIFTS + 1
MESH_ID = pl.DeviceIdType.MESH


def gather_multiply(n_col, meta_ref, a_ref, b_ref, out_ref, A, B, M, run, MS, ktab, ptab, ltab,
                    send_m, recv_m, send_a, recv_a, send_b, recv_b, local_sem):
    row = lax.axis_index("row")
    col = lax.axis_index("col")
    dep = lax.axis_index("depth")
    side = lax.rem(col, 2)
    half = A.shape[2]
    per_row = A.shape[3]
    inner = B.shape[2]
    size = B.shape[3]
    out_cols = out_ref.shape[1] // size
    terms = SHIFTS * 2 * per_row
    zero_at = half * terms

    def at(col_offset, flip_depth=False, flip_row=False):
        return (
            1 - row if flip_row else row,
            lax.rem(col + col_offset + n_col, n_col),
            1 - dep if flip_depth else dep,
        )

    chain_dev = at(-2)
    twin_dev = at(0, True)
    row_dev = at(0, False, True)
    side_dev = (row, col + 1 - 2 * side, dep)

    barrier = pltpu.get_barrier_semaphore()
    reach = REACH - 1
    offsets = [o for o in range(1, n_col) if o <= reach or n_col - o <= reach]
    peers = [at(o, flip) for o in offsets for flip in (False, True)]
    peers += [twin_dev, row_dev, at(0, True, True)]
    for peer in peers:
        pl.semaphore_signal(barrier, inc=1, device_id=peer, device_id_type=MESH_ID)
    pl.semaphore_wait(barrier, len(peers))

    def remote(src, dst, ssem, rsem, dev):
        return pltpu.make_async_remote_copy(
            src_ref=src, dst_ref=dst, send_sem=ssem, recv_sem=rsem, device_id=dev, device_id_type=MESH_ID
        )

    meta_copies = []
    for q in range(REACH):
        for d in range(2):
            slot = q * 2 + d
            if slot:
                meta_copies.append(
                    remote(meta_ref, M.at[slot], send_m.at[slot], recv_m.at[slot], at(-q, d == 1))
                )
    for d in range(2):
        slot = REACH * 2 + d
        meta_copies.append(
            remote(meta_ref, M.at[slot], send_m.at[slot], recv_m.at[slot], at(0, d == 1, True))
        )
    for copy in meta_copies:
        copy.start()
    meta_local = pltpu.make_async_copy(meta_ref, M.at[0], local_sem.at[0])
    meta_local.start()

    own_a = a_ref.at[pl.ds(dep * half, half)]
    swap = remote(a_ref.at[pl.ds((1 - dep) * half, half)], A.at[0, 1], send_a.at[0], recv_a.at[0, 1], twin_dev)
    chain = [
        remote(src, A.at[2, d], send_a.at[1 + d], recv_a.at[2, d], chain_dev)
        for d, src in enumerate((own_a, A.at[0, 1]))
    ]
    chain2 = [
        remote(A.at[2, d], A.at[4, d], send_a.at[3 + d], recv_a.at[4, d], chain_dev) for d in range(2)
    ]
    odd1 = [
        remote(src, A.at[1, d], send_a.at[5 + d], recv_a.at[1, d], side_dev)
        for d, src in enumerate((own_a, A.at[0, 1]))
    ]
    odd3 = [remote(A.at[2, d], A.at[3, d], send_a.at[7 + d], recv_a.at[3, d], side_dev) for d in range(2)]
    even1 = [remote(A.at[2, d], A.at[1, d], send_a.at[5 + d], recv_a.at[1, d], side_dev) for d in range(2)]
    even3 = [remote(A.at[4, d], A.at[3, d], send_a.at[7 + d], recv_a.at[3, d], side_dev) for d in range(2)]
    a_local = pltpu.make_async_copy(own_a, A.at[0, 0], local_sem.at[1])

    far_b, near_b, pass_b, b_local = [], [], [], []
    for k in range(SHIFTS // 2):
        s_far = lax.rem(col + 1, 2) + 2 * k
        m_far = lax.rem(1 - row + col + s_far, n_col) // 2
        far_b.append(remote(b_ref.at[m_far], B.at[0, s_far], send_b.at[k], recv_b.at[0, s_far], row_dev))
        s_near = side + 2 * k
        m_near = lax.rem(row + col + s_near, n_col) // 2
        near_b.append(remote(b_ref.at[m_near], B.at[1, s_near], send_b.at[2 + k], recv_b.at[1, s_near], twin_dev))
        b_local.append(pltpu.make_async_copy(b_ref.at[m_near], B.at[0, s_near], local_sem.at[2 + k]))
        pass_b.append(remote(B.at[0, s_far], B.at[1, s_far], send_b.at[4 + k], recv_b.at[1, s_far], twin_dev))

    swap.start()
    chain[0].start()
    far_b[0].start()

    @pl.when(side == 1)
    def _():
        odd1[0].start()

    far_b[1].start()
    for copy in near_b:
        copy.start()
    a_local.start()
    for copy in b_local:
        copy.start()

    swap.wait_recv()
    chain[1].start()

    @pl.when(side == 1)
    def _():
        odd1[1].start()

    run[zero_at] = jnp.zeros(run.shape[1:], jnp.float32)
    meta_local.wait()
    for copy in meta_copies:
        copy.wait_recv()
    to_scalars = pltpu.make_async_copy(M, MS, local_sem.at[4])
    to_scalars.start()
    to_scalars.wait()

    def tables(r, carry):
        cs = []
        for s in range(SHIFTS):
            slot_b = lax.rem(row + col + s, n_col) // 2
            near = lax.rem(col + s, 2) == 0
            for d in range(2):
                m_at = jnp.where(near, d, REACH * 2 + d)
                for t in range(per_row):
                    k = MS[(s + row) * 2 + d, 0, (dep * half + r) * per_row + t]
                    kk = jnp.maximum(k, 0)
                    c = MS[m_at, 0, 2 * half * per_row + slot_b * inner + kk]
                    c = jnp.where(k >= 0, c, -1)
                    here = r * terms + len(cs)
                    before = jnp.int32(zero_at)
                    for at_p, c_p in enumerate(cs):
                        before = jnp.where(c_p == c, r * terms + at_p, before)
                    ktab[here] = kk
                    ptab[here] = before
                    cs.append(c)
        for c in range(out_cols):
            last = jnp.int32(zero_at)
            for at_p, c_p in enumerate(cs):
                last = jnp.where(c_p == c, r * terms + at_p, last)
            ltab[r * out_cols + c] = last
        return carry

    lax.fori_loop(0, half, tables, 0)

    for d in range(2):
        chain[d].wait_recv()
        chain2[d].start()

        @pl.when(side == 0)
        def _():
            even1[d].start()

        @pl.when(side == 1)
        def _():
            odd3[d].start()

    far_b[0].wait_recv()
    pass_b[0].start()
    for d in range(2):
        chain2[d].wait_recv()

        @pl.when(side == 0)
        def _():
            even3[d].start()

    far_b[1].wait_recv()
    pass_b[1].start()

    a_local.wait()
    for copy in b_local:
        copy.wait()
    for copy in near_b:
        copy.wait_recv()
    for d in range(2):
        odd1[d].wait_recv()
    for copy in pass_b:
        copy.wait_recv()
    for d in range(2):
        odd3[d].wait_recv()

    def products(step, carry):
        s = step // 2
        d = lax.rem(step, 2)
        for t in range(per_row):
            for r in range(half):
                here = r * terms + step * per_row + t
                value = jnp.dot(
                    A[s + row, d, r, t], B[d, s, ktab[here]], preferred_element_type=jnp.float32
                )
                run[here] = value + run[ptab[here]]
        return carry

    lax.fori_loop(0, SHIFTS * 2, products, 0)

    def place(r, carry):
        rows = pl.ds(pl.multiple_of(r * size, size), size)
        for c in range(out_cols):
            out_ref[rows, c * size : (c + 1) * size] = run[ltab[r * out_cols + c]].astype(out_ref.dtype)
        return carry

    lax.fori_loop(0, half, place, 0)

    for copy in meta_copies + [swap] + chain + chain2 + odd1 + odd3 + far_b + near_b + pass_b:
        copy.wait_send()


def local_fast(n_col, a_tiles, a_cols, a_count, b_tiles, b_cols, b_count):
    block_rows, per_row, size = a_tiles.shape[2:5]
    slots, inner = b_tiles.shape[0], b_tiles.shape[4]
    half = block_rows // 2
    t_ids = lax.broadcasted_iota(jnp.int32, (block_rows, per_row), 1)
    a_meta = jnp.where(t_ids < a_count.reshape(block_rows, 1), a_cols.reshape(block_rows, per_row), -1)
    b_meta = jnp.where(b_count.reshape(slots * inner) > 0, b_cols.reshape(slots * inner), -1)
    flat = jnp.concatenate([a_meta.reshape(-1), b_meta])
    width = -(-flat.shape[0] // 128) * 128
    meta = jnp.broadcast_to(jnp.pad(flat, (0, width - flat.shape[0]))[None, :], (8, width))
    terms = SHIFTS * 2 * per_row
    count = half * terms
    metas = REACH * 2 + 2
    any_spec = pl.BlockSpec(memory_space=pl.ANY)
    vmem_spec = pl.BlockSpec(memory_space=pltpu.VMEM)
    return pl.pallas_call(
        functools.partial(gather_multiply, n_col),
        out_shape=jax.ShapeDtypeStruct((half * size, BC * size), jnp.bfloat16),
        in_specs=[vmem_spec, any_spec, any_spec],
        out_specs=vmem_spec,
        scratch_shapes=[
            pltpu.VMEM((REACH, 2, half, per_row, size, size), jnp.bfloat16),
            pltpu.VMEM((2, SHIFTS, inner, size, size), jnp.bfloat16),
            pltpu.VMEM((metas, 8, width), jnp.int32),
            pltpu.VMEM((count + 1, size, size), jnp.float32),
            pltpu.SMEM((metas, 8, width), jnp.int32),
            pltpu.SMEM((count,), jnp.int32),
            pltpu.SMEM((count,), jnp.int32),
            pltpu.SMEM((half * BC,), jnp.int32),
            pltpu.SemaphoreType.DMA((metas,)),
            pltpu.SemaphoreType.DMA((metas,)),
            pltpu.SemaphoreType.DMA((9,)),
            pltpu.SemaphoreType.DMA((REACH, 2)),
            pltpu.SemaphoreType.DMA((6,)),
            pltpu.SemaphoreType.DMA((2, SHIFTS)),
            pltpu.SemaphoreType.DMA((5,)),
        ],
        compiler_params=pltpu.CompilerParams(
            collective_id=0, has_side_effects=True, vmem_limit_bytes=40 * 1024 * 1024
        ),
    )(meta, a_tiles.reshape(block_rows, per_row, size, size), b_tiles.reshape(slots, inner, size, size))


def solution(mesh):
    placed = (
        P("row", ("col", "depth"), None, None, None, None),
        P("row", ("col", "depth"), None, None),
        P("row", ("col", "depth"), None),
        P(None, "row", "depth", "col", None, None, None, None),
        P(None, "row", "depth", "col", None, None),
        P(None, "row", "depth", "col", None),
    )
    n_col = mesh.shape["col"]
    if mesh.shape["row"] == 2 and mesh.shape["depth"] == 2 and n_col % 2 == 0 and n_col > SHIFTS:
        body = functools.partial(local_fast, n_col)
    else:
        body = local
    return jax.shard_map(
        body, mesh=mesh, in_specs=placed, out_specs=P(("row", "depth"), "col"), check_vma=False
    )
```

```python
import functools
import math

import jax
import jax.numpy as jnp
from jax import lax
from jax.experimental import pallas as pl
from jax.experimental.pallas import tpu as pltpu
from jax.sharding import PartitionSpec as P

BC = 12
SHIFTS = 4


def for_sending(array):
    return jax.tree.map(lambda a: a.astype(jnp.bfloat16) if a.dtype == jnp.float32 else a, array)


def shifted(value, axis, steps):
    count = lax.axis_size(axis)
    pairs = [(source, (source + steps) % count) for source in range(count)]
    return lax.ppermute(value, axis, pairs)


def dense_panel(tiles_b, cols_b, count_b, width):
    slot_ids = lax.broadcasted_iota(jnp.int32, cols_b.shape, 1)
    valid_slot = slot_ids < count_b[:, None]
    targets = lax.broadcasted_iota(jnp.int32, (1, 1, width), 2)
    placing = jnp.logical_and(cols_b[:, :, None] == targets, valid_slot[:, :, None]).astype(
        jnp.bfloat16
    )
    spread = jnp.einsum("kuc,kuab->kacb", placing, tiles_b, preferred_element_type=jnp.float32)
    inner_blocks = tiles_b.shape[0]
    tile_size = tiles_b.shape[2]
    return spread.astype(jnp.bfloat16).reshape(inner_blocks, tile_size, width * tile_size)


def panel_product(tiles_a, cols_a, count_a, rows_dense):
    block_rows = tiles_a.shape[0]
    per_row = tiles_a.shape[1]
    tile_size = tiles_a.shape[2]
    slot_ids = lax.broadcasted_iota(jnp.int32, cols_a.shape, 1)
    valid_slot = slot_ids < count_a[:, None]
    masked = jnp.where(valid_slot[:, :, None, None], tiles_a, jnp.zeros_like(tiles_a))
    group_rows = math.gcd(block_rows, 4)

    def one_group(pieces):
        tiles_part, cols_part = pieces
        chosen = jnp.take(rows_dense, cols_part, axis=0)
        return jnp.einsum("rtab,rtbn->ran", tiles_part, chosen, preferred_element_type=jnp.float32)

    grouped = lax.map(
        one_group,
        (
            masked.reshape(block_rows // group_rows, group_rows, per_row, tile_size, tile_size),
            cols_a.reshape(block_rows // group_rows, group_rows, per_row),
        ),
    )
    return grouped.reshape(block_rows, tile_size, rows_dense.shape[2])


def roll_slots(stack, offset):
    slot_total = stack[0].shape[0]
    return tuple(
        (
            lax.dynamic_slice_in_dim(
                jnp.concatenate([member, member], 0), offset % slot_total, slot_total, 0
            )
            for member in stack
        )
    )


def select_if(flag, fresh, stale):
    return tuple((jnp.where(flag, new_part, old_part) for new_part, old_part in zip(fresh, stale)))


def local(a_tiles, a_cols, a_count, b_tiles, b_cols, b_count):
    rows_axis = lax.axis_size("row")
    cols_axis = lax.axis_size("col")
    row_group = lax.axis_index("row")
    col_group = lax.axis_index("col")
    tiles_a = a_tiles[0, 0]
    cols_a = a_cols[0, 0]
    count_a = a_count[0, 0]
    tiles_b = b_tiles[:, 0, 0, 0]
    cols_b = b_cols[:, 0, 0, 0]
    count_b = b_count[:, 0, 0, 0]
    for bit_pos in range((rows_axis - 1).bit_length()):
        stride = 1 << bit_pos
        moved = (
            shifted(tiles_a, "col", cols_axis - stride),
            shifted(for_sending(cols_a), "col", cols_axis - stride).astype(cols_a.dtype),
            shifted(for_sending(count_a), "col", cols_axis - stride).astype(count_a.dtype),
        )
        tiles_a, cols_a, count_a = select_if(
            row_group // stride % 2 == 1, moved, (tiles_a, cols_a, count_a)
        )
    for bit_pos in range((cols_axis - 1).bit_length()):
        stride = 1 << bit_pos
        nearby = stride % rows_axis
        if nearby:
            moved = (
                shifted(tiles_b, "row", rows_axis - nearby),
                shifted(for_sending(cols_b), "row", rows_axis - nearby).astype(cols_b.dtype),
                shifted(for_sending(count_b), "row", rows_axis - nearby).astype(count_b.dtype),
            )
        else:
            moved = (tiles_b, cols_b, count_b)
        moved = roll_slots(moved, (row_group + stride) // rows_axis)
        tiles_b, cols_b, count_b = select_if(
            col_group // stride % 2 == 1, moved, (tiles_b, cols_b, count_b)
        )
    tile_size = tiles_a.shape[2]
    running = jnp.zeros((tiles_a.shape[0], tile_size, BC * tile_size), jnp.float32)
    for turn_no in range(SHIFTS):
        current_tiles = tiles_b[0]
        current_cols = cols_b[0]
        current_count = count_b[0]
        rows_dense = dense_panel(current_tiles, current_cols, current_count, BC)
        running = running + panel_product(tiles_a, cols_a, count_a, rows_dense)
        if turn_no + 1 < SHIFTS:
            tiles_a, cols_a, count_a = (
                shifted(tiles_a, "col", cols_axis - 1),
                shifted(for_sending(cols_a), "col", cols_axis - 1).astype(cols_a.dtype),
                shifted(for_sending(count_a), "col", cols_axis - 1).astype(count_a.dtype),
            )
            moved = (
                shifted(tiles_b, "row", rows_axis - 1),
                shifted(for_sending(cols_b), "row", rows_axis - 1).astype(cols_b.dtype),
                shifted(for_sending(count_b), "row", rows_axis - 1).astype(count_b.dtype),
            )
            tiles_b, cols_b, count_b = roll_slots(moved, (row_group + 1) // rows_axis)
    flat_running = running.reshape(-1, running.shape[2])
    summed = lax.psum(flat_running, "depth")
    half_rows = flat_running.shape[0] // lax.axis_size("depth")
    own_rows = lax.dynamic_slice_in_dim(summed, lax.axis_index("depth") * half_rows, half_rows, 0)
    return own_rows.astype(jnp.bfloat16)


REACH = SHIFTS + 1
CHUNKS = 4
MESH_ID = pl.DeviceIdType.MESH


def gather_multiply(n_col, a_cols, a_count, b_cols, b_count, a_ref, b_ref, out_ref, A, Bn0, Bn1, Bf0, Bf1,
                    Gn0, Gn1, Gf0, Gf1, MA, MC, MB, MK, SA, SC, SB, SK, run, ktab, ptab, ltab,
                    send_m, recv_m, send_a, recv_a, send_b, recv_b, local_sem):
    row = lax.axis_index("row")
    col = lax.axis_index("col")
    dep = lax.axis_index("depth")
    side = lax.rem(col, 2)
    half = A.shape[2]
    per_row = A.shape[3]
    size = A.shape[4]
    inner = Bn0.shape[0]
    out_cols = out_ref.shape[1] // size
    terms = SHIFTS * 2 * per_row
    zero_at = half * terms
    units = [(d, r) for d in range(2) for r in range(half)]
    count_u = len(units)
    step_b = inner // CHUNKS

    def at(col_offset, flip_depth=False, flip_row=False):
        return (
            1 - row if flip_row else row,
            lax.rem(col + col_offset + n_col, n_col),
            1 - dep if flip_depth else dep,
        )

    chain_dev = at(-2)
    twin_dev = at(0, True)
    row_dev = at(0, False, True)
    side_dev = (row, col + 1 - 2 * side, dep)

    def remote(src, dst, ssem, rsem, dev):
        return pltpu.make_async_remote_copy(
            src_ref=src, dst_ref=dst, send_sem=ssem, recv_sem=rsem, device_id=dev, device_id_type=MESH_ID
        )

    s_near = [side + 2 * k for k in range(2)]
    s_far = [1 - side + 2 * k for k in range(2)]
    m_near = [lax.rem(row + col + s, n_col) // 2 for s in s_near]
    m_far = [lax.rem(1 - row + col + s, n_col) // 2 for s in s_far]
    m_mine = [lax.rem(row + col + s, n_col) // 2 for s in s_far]
    near_own, near_twin = (Bn0, Bn1), (Gn0, Gn1)
    far_own, far_twin = (Bf0, Bf1), (Gf0, Gf1)
    index_local = [
        pltpu.make_async_copy(src, dst.at[0], local_sem.at[n])
        for n, (src, dst) in enumerate(((a_cols, MA), (a_count, MC), (b_cols, MB), (b_count, MK)))
    ]
    b_local = [pltpu.make_async_copy(b_ref.at[m_near[k]], near_own[k], local_sem.at[4 + k]) for k in range(2)]
    a_local = pltpu.make_async_copy(a_ref.at[pl.ds(dep * half, half)], A.at[0, 0], local_sem.at[6])
    for copy in index_local + b_local + [a_local]:
        copy.start()

    barrier = pltpu.get_barrier_semaphore()
    reach = REACH - 1
    offsets = [o for o in range(1, n_col) if o <= reach or n_col - o <= reach]
    peers = [at(o, flip) for o in offsets for flip in (False, True)]
    peers += [twin_dev, row_dev, at(0, True, True)]
    for peer in peers:
        pl.semaphore_signal(barrier, inc=1, device_id=peer, device_id_type=MESH_ID)
    pl.semaphore_wait(barrier, len(peers))

    index_copies = []
    for q in range(REACH):
        for d in range(2):
            slot = q * 2 + d
            if slot:
                for n, (src, dst) in enumerate(((a_cols, MA), (a_count, MC))):
                    index_copies.append(
                        remote(src, dst.at[slot], send_m.at[n, slot], recv_m.at[n, slot], at(-q, d == 1))
                    )
    for slot in range(1, 4):
        for n, (src, dst) in enumerate(((b_cols, MB), (b_count, MK))):
            index_copies.append(
                remote(
                    src, dst.at[slot], send_m.at[2 + n, slot], recv_m.at[2 + n, slot],
                    at(0, slot % 2 == 1, slot >= 2),
                )
            )

    swap = [
        remote(a_ref.at[(1 - dep) * half + r], A.at[0, 1, r], send_a.at[0, r], recv_a.at[0, half + r], twin_dev)
        for r in range(half)
    ]
    first = [a_ref.at[dep * half + r] for r in range(half)] + [A.at[0, 1, r] for r in range(half)]

    def to_panel(p, sources, send_row, dev):
        return [
            remote(src, A.at[p, d, r], send_a.at[send_row, u], recv_a.at[p, u], dev)
            for u, ((d, r), src) in enumerate(zip(units, sources))
        ]

    def panel(p):
        return [A.at[p, d, r] for d, r in units]

    chain = to_panel(2, first, 1, chain_dev)
    chain2 = to_panel(4, panel(2), 2, chain_dev)
    odd1 = to_panel(1, first, 3, side_dev)
    odd3 = to_panel(3, panel(2), 4, side_dev)
    even1 = to_panel(1, panel(2), 3, side_dev)
    even3 = to_panel(3, panel(4), 4, side_dev)

    near_b = [
        remote(b_ref.at[m_near[k]], near_twin[k], send_b.at[2 * k, CHUNKS], recv_b.at[2 * k, CHUNKS], twin_dev)
        for k in range(2)
    ]
    far_b, pass_b = [], []
    for k in range(2):
        for c in range(CHUNKS):
            part = pl.ds(c * step_b, step_b)
            far_b.append(
                remote(
                    b_ref.at[m_far[k], part], far_own[k].at[part],
                    send_b.at[2 * k, c], recv_b.at[2 * k, c], row_dev,
                )
            )
            pass_b.append(
                remote(
                    far_own[k].at[part], far_twin[k].at[part],
                    send_b.at[2 * k + 1, c], recv_b.at[2 * k + 1, c], twin_dev,
                )
            )

    for copy in index_copies[:2] + index_copies[-6:]:
        copy.start()
    for copy in index_copies[2:-6]:
        copy.start()
    for r in range(half):
        chain[r].start()
        swap[r].start()

        @pl.when(side == 1)
        def _():
            odd1[r].start()

    for copy in far_b:
        copy.start()
    for copy in near_b:
        copy.start()
    run[zero_at] = jnp.zeros(run.shape[1:], jnp.float32)
    for r in range(half):
        swap[r].wait_recv()
        chain[half + r].start()

        @pl.when(side == 1)
        def _():
            odd1[half + r].start()

    groups = [(s, m, k, d, far) for k in range(2) for far, s, m in ((0, s_near[k], m_near[k]), (1, s_far[k], m_mine[k]))
              for d in range(2)]

    def tables(r, carry):
        cs = []
        for s, m, _, d, far in groups:
            slot = (s + row) * 2 + d
            used = SC[slot, 0, dep * half + r]
            for t in range(per_row):
                k = SA[slot, t, dep * half + r]
                c = SB[2 * far + d, m, 0, k]
                ok = jnp.logical_and(used > t, SK[2 * far + d, m, 0, k] > 0)
                c = jnp.where(ok, c, -1)
                here = r * terms + len(cs)
                before = jnp.int32(zero_at)
                for at_p, c_p in enumerate(cs):
                    before = jnp.where(c_p == c, r * terms + at_p, before)
                ktab[here] = k
                ptab[here] = before
                cs.append(c)
        for c in range(out_cols):
            last = jnp.int32(zero_at)
            for at_p, c_p in enumerate(cs):
                last = jnp.where(c_p == c, r * terms + at_p, last)
            ltab[r * out_cols + c] = last
        return carry

    def product(g, d, r, t, right):
        here = r * terms + g * per_row + t
        value = jnp.dot(A[groups[g][0] + row, d, r, t], right[ktab[here]], preferred_element_type=jnp.float32)
        run[here] = value + run[ptab[here]]

    def whole_group(g, right):
        d = groups[g][3]

        def one(t, carry):
            for r in range(half):
                product(g, d, r, t, right)
            return carry

        lax.fori_loop(0, per_row, one, 0)

    for u in range(count_u):
        chain[u].wait_recv()
        chain2[u].start()

        @pl.when(side == 0)
        def _():
            even1[u].start()

        @pl.when(side == 1)
        def _():
            odd3[u].start()

        if u % 2 == 1 and u // 2 < CHUNKS:
            far_b[u // 2].wait_recv()
            pass_b[u // 2].start()
        if u == 1:
            for copy in index_local:
                copy.wait()
            for copy in index_copies:
                copy.wait_recv()
            scalars = [
                pltpu.make_async_copy(src, dst, local_sem.at[n])
                for n, (src, dst) in enumerate(((MA, SA), (MC, SC), (MB, SB), (MK, SK)))
            ]
            for copy in scalars:
                copy.start()
            for copy in scalars:
                copy.wait()
        if 2 <= u < 2 + half:
            tables(u - 2, 0)

    def near_unit(u):
        odd3[u].wait_recv()
        d, r = units[u]
        for t in range(per_row):
            product(4 + d, d, r, t, (Bn1, Gn1)[d])

    done = 0
    for u in range(count_u):
        chain2[u].wait_recv()

        @pl.when(side == 0)
        def _():
            even3[u].start()

        if u % 2 == 1 and u // 2 < CHUNKS:
            far_b[CHUNKS + u // 2].wait_recv()
            pass_b[CHUNKS + u // 2].start()
        if u == 2:
            a_local.wait()
            for copy in b_local:
                copy.wait()
            for copy in near_b:
                copy.wait_recv()
            for copy in odd1:
                copy.wait_recv()
            for c in range(CHUNKS):
                pass_b[c].wait_recv()
        if 2 <= u < 6:
            whole_group(u - 2, (Bn0, Gn0, Bf0, Gf0)[u - 2])
        if u >= 5:
            near_unit(done)
            done += 1
    for u in range(done, count_u):
        near_unit(u)
    whole_group(6, Bf1)
    for c in range(CHUNKS):
        pass_b[CHUNKS + c].wait_recv()
    whole_group(7, Gf1)

    def place(r, carry):
        rows = pl.ds(pl.multiple_of(r * size, size), size)
        for c in range(out_cols):
            out_ref[rows, c * size : (c + 1) * size] = run[ltab[r * out_cols + c]].astype(out_ref.dtype)
        return carry

    lax.fori_loop(0, half, place, 0)

    for copy in index_copies + swap + chain + chain2 + odd1 + odd3 + far_b + near_b + pass_b:
        copy.wait_send()


def local_fast(n_col, a_tiles, a_cols, a_count, b_tiles, b_cols, b_count):
    block_rows, per_row, size = a_tiles.shape[2:5]
    slots, inner = b_tiles.shape[0], b_tiles.shape[4]
    half = block_rows // 2
    terms = SHIFTS * 2 * per_row
    count = half * terms
    panels = REACH * 2
    hbm = pl.BlockSpec(memory_space=pltpu.HBM)
    vmem = pl.BlockSpec(memory_space=pltpu.VMEM)
    index_shapes = [(panels, per_row, block_rows), (panels, 1, block_rows), (4, slots, 1, inner), (4, slots, 1, inner)]
    right = pltpu.VMEM((inner, size, size), jnp.bfloat16)
    return pl.pallas_call(
        functools.partial(gather_multiply, n_col),
        out_shape=jax.ShapeDtypeStruct((half * size, BC * size), jnp.bfloat16),
        in_specs=[hbm] * 6,
        out_specs=vmem,
        scratch_shapes=[pltpu.VMEM((REACH, 2, half, per_row, size, size), jnp.bfloat16)]
        + [right] * 8
        + [pltpu.VMEM(shape, jnp.int32) for shape in index_shapes]
        + [pltpu.SMEM(shape, jnp.int32) for shape in index_shapes]
        + [
            pltpu.VMEM((count + 1, size, size), jnp.float32),
            pltpu.SMEM((count,), jnp.int32),
            pltpu.SMEM((count,), jnp.int32),
            pltpu.SMEM((half * BC,), jnp.int32),
            pltpu.SemaphoreType.DMA((4, panels)),
            pltpu.SemaphoreType.DMA((4, panels)),
            pltpu.SemaphoreType.DMA((5, 2 * half)),
            pltpu.SemaphoreType.DMA((REACH, 2 * half)),
            pltpu.SemaphoreType.DMA((4, CHUNKS + 1)),
            pltpu.SemaphoreType.DMA((4, CHUNKS + 1)),
            pltpu.SemaphoreType.DMA((7,)),
        ],
        compiler_params=pltpu.CompilerParams(
            collective_id=0, has_side_effects=True, vmem_limit_bytes=65200000
        ),
    )(
        jnp.swapaxes(a_cols.reshape(block_rows, per_row), 0, 1),
        a_count.reshape(1, block_rows),
        b_cols.reshape(slots, 1, inner),
        b_count.reshape(slots, 1, inner),
        a_tiles.reshape(block_rows, per_row, size, size),
        b_tiles.reshape(slots, inner, size, size),
    )


def solution(mesh):
    placed = (
        P("row", ("col", "depth"), None, None, None, None),
        P("row", ("col", "depth"), None, None),
        P("row", ("col", "depth"), None),
        P(None, "row", "depth", "col", None, None, None, None),
        P(None, "row", "depth", "col", None, None),
        P(None, "row", "depth", "col", None),
    )
    n_col = mesh.shape["col"]
    if mesh.shape["row"] == 2 and mesh.shape["depth"] == 2 and n_col % 2 == 0 and n_col > SHIFTS:
        body = functools.partial(local_fast, n_col)
    else:
        body = local
    return jax.shard_map(
        body, mesh=mesh, in_specs=placed, out_specs=P(("row", "depth"), "col"), check_vma=False
    )
```

```python
import functools
import math

import jax
import jax.numpy as jnp
from jax import lax
from jax.experimental import pallas as pl
from jax.experimental.pallas import tpu as pltpu
from jax.sharding import PartitionSpec as P

BC = 12
SHIFTS = 4


def for_sending(array):
    return jax.tree.map(lambda a: a.astype(jnp.bfloat16) if a.dtype == jnp.float32 else a, array)


def shifted(value, axis, steps):
    count = lax.axis_size(axis)
    pairs = [(source, (source + steps) % count) for source in range(count)]
    return lax.ppermute(value, axis, pairs)


def dense_panel(tiles_b, cols_b, count_b, width):
    slot_ids = lax.broadcasted_iota(jnp.int32, cols_b.shape, 1)
    valid_slot = slot_ids < count_b[:, None]
    targets = lax.broadcasted_iota(jnp.int32, (1, 1, width), 2)
    placing = jnp.logical_and(cols_b[:, :, None] == targets, valid_slot[:, :, None]).astype(
        jnp.bfloat16
    )
    spread = jnp.einsum("kuc,kuab->kacb", placing, tiles_b, preferred_element_type=jnp.float32)
    inner_blocks = tiles_b.shape[0]
    tile_size = tiles_b.shape[2]
    return spread.astype(jnp.bfloat16).reshape(inner_blocks, tile_size, width * tile_size)


def panel_product(tiles_a, cols_a, count_a, rows_dense):
    block_rows = tiles_a.shape[0]
    per_row = tiles_a.shape[1]
    tile_size = tiles_a.shape[2]
    slot_ids = lax.broadcasted_iota(jnp.int32, cols_a.shape, 1)
    valid_slot = slot_ids < count_a[:, None]
    masked = jnp.where(valid_slot[:, :, None, None], tiles_a, jnp.zeros_like(tiles_a))
    group_rows = math.gcd(block_rows, 4)

    def one_group(pieces):
        tiles_part, cols_part = pieces
        chosen = jnp.take(rows_dense, cols_part, axis=0)
        return jnp.einsum("rtab,rtbn->ran", tiles_part, chosen, preferred_element_type=jnp.float32)

    grouped = lax.map(
        one_group,
        (
            masked.reshape(block_rows // group_rows, group_rows, per_row, tile_size, tile_size),
            cols_a.reshape(block_rows // group_rows, group_rows, per_row),
        ),
    )
    return grouped.reshape(block_rows, tile_size, rows_dense.shape[2])


def roll_slots(stack, offset):
    slot_total = stack[0].shape[0]
    return tuple(
        (
            lax.dynamic_slice_in_dim(
                jnp.concatenate([member, member], 0), offset % slot_total, slot_total, 0
            )
            for member in stack
        )
    )


def select_if(flag, fresh, stale):
    return tuple((jnp.where(flag, new_part, old_part) for new_part, old_part in zip(fresh, stale)))


def local(a_tiles, a_cols, a_count, b_tiles, b_cols, b_count):
    rows_axis = lax.axis_size("row")
    cols_axis = lax.axis_size("col")
    row_group = lax.axis_index("row")
    col_group = lax.axis_index("col")
    tiles_a = a_tiles[0, 0]
    cols_a = a_cols[0, 0]
    count_a = a_count[0, 0]
    tiles_b = b_tiles[:, 0, 0, 0]
    cols_b = b_cols[:, 0, 0, 0]
    count_b = b_count[:, 0, 0, 0]
    for bit_pos in range((rows_axis - 1).bit_length()):
        stride = 1 << bit_pos
        moved = (
            shifted(tiles_a, "col", cols_axis - stride),
            shifted(for_sending(cols_a), "col", cols_axis - stride).astype(cols_a.dtype),
            shifted(for_sending(count_a), "col", cols_axis - stride).astype(count_a.dtype),
        )
        tiles_a, cols_a, count_a = select_if(
            row_group // stride % 2 == 1, moved, (tiles_a, cols_a, count_a)
        )
    for bit_pos in range((cols_axis - 1).bit_length()):
        stride = 1 << bit_pos
        nearby = stride % rows_axis
        if nearby:
            moved = (
                shifted(tiles_b, "row", rows_axis - nearby),
                shifted(for_sending(cols_b), "row", rows_axis - nearby).astype(cols_b.dtype),
                shifted(for_sending(count_b), "row", rows_axis - nearby).astype(count_b.dtype),
            )
        else:
            moved = (tiles_b, cols_b, count_b)
        moved = roll_slots(moved, (row_group + stride) // rows_axis)
        tiles_b, cols_b, count_b = select_if(
            col_group // stride % 2 == 1, moved, (tiles_b, cols_b, count_b)
        )
    tile_size = tiles_a.shape[2]
    running = jnp.zeros((tiles_a.shape[0], tile_size, BC * tile_size), jnp.float32)
    for turn_no in range(SHIFTS):
        current_tiles = tiles_b[0]
        current_cols = cols_b[0]
        current_count = count_b[0]
        rows_dense = dense_panel(current_tiles, current_cols, current_count, BC)
        running = running + panel_product(tiles_a, cols_a, count_a, rows_dense)
        if turn_no + 1 < SHIFTS:
            tiles_a, cols_a, count_a = (
                shifted(tiles_a, "col", cols_axis - 1),
                shifted(for_sending(cols_a), "col", cols_axis - 1).astype(cols_a.dtype),
                shifted(for_sending(count_a), "col", cols_axis - 1).astype(count_a.dtype),
            )
            moved = (
                shifted(tiles_b, "row", rows_axis - 1),
                shifted(for_sending(cols_b), "row", rows_axis - 1).astype(cols_b.dtype),
                shifted(for_sending(count_b), "row", rows_axis - 1).astype(count_b.dtype),
            )
            tiles_b, cols_b, count_b = roll_slots(moved, (row_group + 1) // rows_axis)
    flat_running = running.reshape(-1, running.shape[2])
    summed = lax.psum(flat_running, "depth")
    half_rows = flat_running.shape[0] // lax.axis_size("depth")
    own_rows = lax.dynamic_slice_in_dim(summed, lax.axis_index("depth") * half_rows, half_rows, 0)
    return own_rows.astype(jnp.bfloat16)


REACH = SHIFTS + 1
CHUNKS = 4
WIDTH = 1
MESH_ID = pl.DeviceIdType.MESH


def gather_multiply(n_col, a_cols, a_count, b_cols, b_count, a_ref, b_ref, out_ref, A, Bn0, Bn1, Bf0, Bf1,
                    Gn0, Gn1, Gf0, Gf1, MA, MC, MB, MK, SA, SC, SB, SK, run, ktab, ptab, ltab,
                    send_m, recv_m, send_a, recv_a, send_b, recv_b, local_sem):
    row = lax.axis_index("row")
    col = lax.axis_index("col")
    dep = lax.axis_index("depth")
    side = lax.rem(col, 2)
    half = A.shape[2]
    per_row = A.shape[3]
    size = A.shape[4]
    inner = Bn0.shape[0]
    out_cols = out_ref.shape[1] // size
    terms = SHIFTS * 2 * per_row
    zero_at = half * terms
    parts = half // WIDTH
    units = [(d, pl.ds(h * WIDTH, WIDTH)) for d in range(2) for h in range(parts)]
    count_u = len(units)
    step_b = inner // CHUNKS

    def at(col_offset, flip_depth=False, flip_row=False):
        return (
            1 - row if flip_row else row,
            lax.rem(col + col_offset + n_col, n_col),
            1 - dep if flip_depth else dep,
        )

    chain_dev = at(-2)
    twin_dev = at(0, True)
    row_dev = at(0, False, True)
    side_dev = (row, col + 1 - 2 * side, dep)

    def remote(src, dst, ssem, rsem, dev):
        return pltpu.make_async_remote_copy(
            src_ref=src, dst_ref=dst, send_sem=ssem, recv_sem=rsem, device_id=dev, device_id_type=MESH_ID
        )

    s_near = [side + 2 * k for k in range(2)]
    s_far = [1 - side + 2 * k for k in range(2)]
    m_near = [lax.rem(row + col + s, n_col) // 2 for s in s_near]
    m_far = [lax.rem(1 - row + col + s, n_col) // 2 for s in s_far]
    m_mine = [lax.rem(row + col + s, n_col) // 2 for s in s_far]
    near_own, near_twin = (Bn0, Bn1), (Gn0, Gn1)
    far_own, far_twin = (Bf0, Bf1), (Gf0, Gf1)
    index_local = [
        pltpu.make_async_copy(src, dst.at[0], local_sem.at[n])
        for n, (src, dst) in enumerate(((a_cols, MA), (a_count, MC), (b_cols, MB), (b_count, MK)))
    ]
    b_local = [pltpu.make_async_copy(b_ref.at[m_near[k]], near_own[k], local_sem.at[4 + k]) for k in range(2)]
    a_local = pltpu.make_async_copy(a_ref.at[pl.ds(dep * half, half)], A.at[0, 0], local_sem.at[6])
    for copy in index_local + b_local + [a_local]:
        copy.start()

    barrier = pltpu.get_barrier_semaphore()
    reach = REACH - 1
    offsets = [o for o in range(1, n_col) if o <= reach or n_col - o <= reach]
    peers = [at(o, flip) for o in offsets for flip in (False, True)]
    peers += [twin_dev, row_dev, at(0, True, True)]
    for peer in peers:
        pl.semaphore_signal(barrier, inc=1, device_id=peer, device_id_type=MESH_ID)
    pl.semaphore_wait(barrier, len(peers))

    index_copies = []
    for q in range(REACH):
        for d in range(2):
            slot = q * 2 + d
            if slot:
                for n, (src, dst) in enumerate(((a_cols, MA), (a_count, MC))):
                    index_copies.append(
                        remote(src, dst.at[slot], send_m.at[n, slot], recv_m.at[n, slot], at(-q, d == 1))
                    )
    for slot in range(1, 4):
        for n, (src, dst) in enumerate(((b_cols, MB), (b_count, MK))):
            index_copies.append(
                remote(
                    src, dst.at[slot], send_m.at[2 + n, slot], recv_m.at[2 + n, slot],
                    at(0, slot % 2 == 1, slot >= 2),
                )
            )

    swap = [
        remote(
            a_ref.at[pl.ds((1 - dep) * half + h * WIDTH, WIDTH)], A.at[0, 1, pl.ds(h * WIDTH, WIDTH)],
            send_a.at[0, h], recv_a.at[0, parts + h], twin_dev,
        )
        for h in range(parts)
    ]
    first = [a_ref.at[pl.ds(dep * half + h * WIDTH, WIDTH)] for h in range(parts)]
    first += [A.at[0, 1, pl.ds(h * WIDTH, WIDTH)] for h in range(parts)]

    def to_panel(p, sources, send_row, dev):
        return [
            remote(src, A.at[p, d, r], send_a.at[send_row, u], recv_a.at[p, u], dev)
            for u, ((d, r), src) in enumerate(zip(units, sources))
        ]

    def panel(p):
        return [A.at[p, d, r] for d, r in units]

    chain = to_panel(2, first, 1, chain_dev)
    chain2 = to_panel(4, panel(2), 2, chain_dev)
    odd1 = to_panel(1, first, 3, side_dev)
    odd3 = to_panel(3, panel(2), 4, side_dev)
    even1 = to_panel(1, panel(2), 3, side_dev)
    even3 = to_panel(3, panel(4), 4, side_dev)

    near_b = [
        remote(b_ref.at[m_near[k]], near_twin[k], send_b.at[2 * k, CHUNKS], recv_b.at[2 * k, CHUNKS], twin_dev)
        for k in range(2)
    ]
    far_b, pass_b = [], []
    for k in range(2):
        for c in range(CHUNKS):
            part = pl.ds(c * step_b, step_b)
            far_b.append(
                remote(
                    b_ref.at[m_far[k], part], far_own[k].at[part],
                    send_b.at[2 * k, c], recv_b.at[2 * k, c], row_dev,
                )
            )
            pass_b.append(
                remote(
                    far_own[k].at[part], far_twin[k].at[part],
                    send_b.at[2 * k + 1, c], recv_b.at[2 * k + 1, c], twin_dev,
                )
            )

    for copy in index_copies[:2] + index_copies[-6:]:
        copy.start()
    for copy in index_copies[2:-6]:
        copy.start()
    for r in range(parts):
        chain[r].start()
        swap[r].start()

        @pl.when(side == 1)
        def _():
            odd1[r].start()

    for copy in far_b:
        copy.start()
    for copy in near_b:
        copy.start()
    run[zero_at] = jnp.zeros(run.shape[1:], jnp.float32)
    for r in range(parts):
        swap[r].wait_recv()
        chain[parts + r].start()

        @pl.when(side == 1)
        def _():
            odd1[parts + r].start()

    groups = [(s, m, k, d, far) for k in range(2) for far, s, m in ((0, s_near[k], m_near[k]), (1, s_far[k], m_mine[k]))
              for d in range(2)]

    def tables(r, carry):
        cs = []
        for s, m, _, d, far in groups:
            slot = (s + row) * 2 + d
            used = SC[slot, 0, dep * half + r]
            for t in range(per_row):
                k = SA[slot, t, dep * half + r]
                c = SB[2 * far + d, m, 0, k]
                ok = jnp.logical_and(used > t, SK[2 * far + d, m, 0, k] > 0)
                c = jnp.where(ok, c, -1)
                here = r * terms + len(cs)
                before = jnp.int32(zero_at)
                for at_p, c_p in enumerate(cs):
                    before = jnp.where(c_p == c, r * terms + at_p, before)
                ktab[here] = k
                ptab[here] = before
                cs.append(c)
        for c in range(out_cols):
            last = jnp.int32(zero_at)
            for at_p, c_p in enumerate(cs):
                last = jnp.where(c_p == c, r * terms + at_p, last)
            ltab[r * out_cols + c] = last
        return carry

    def product(g, d, r, t, right):
        here = r * terms + g * per_row + t
        value = jnp.dot(A[groups[g][0] + row, d, r, t], right[ktab[here]], preferred_element_type=jnp.float32)
        run[here] = value + run[ptab[here]]

    def whole_group(g, right):
        d = groups[g][3]

        def one(t, carry):
            for r in range(half):
                product(g, d, r, t, right)
            return carry

        lax.fori_loop(0, per_row, one, 0)

    begin = count_u // 4
    lag = begin + count_u * 3 // 8
    for u in range(count_u):
        chain[u].wait_recv()
        chain2[u].start()

        @pl.when(side == 0)
        def _():
            even1[u].start()

        @pl.when(side == 1)
        def _():
            odd3[u].start()

        for c in range(u * CHUNKS // count_u, (u + 1) * CHUNKS // count_u):
            far_b[c].wait_recv()
            pass_b[c].start()
        if u == begin:
            for copy in index_local:
                copy.wait()
            for copy in index_copies:
                copy.wait_recv()
            scalars = [
                pltpu.make_async_copy(src, dst, local_sem.at[n])
                for n, (src, dst) in enumerate(((MA, SA), (MC, SC), (MB, SB), (MK, SK)))
            ]
            for copy in scalars:
                copy.start()
            for copy in scalars:
                copy.wait()
        for r in range(half):
            if u == begin + r * count_u // (2 * half):
                tables(r, 0)

    def near_unit(u):
        odd3[u].wait_recv()
        d, h = u // parts, u % parts
        for t in range(per_row):
            for r in range(h * WIDTH, (h + 1) * WIDTH):
                product(4 + d, d, r, t, (Bn1, Gn1)[d])

    done = 0
    for u in range(count_u):
        chain2[u].wait_recv()

        @pl.when(side == 0)
        def _():
            even3[u].start()

        for c in range(CHUNKS + u * CHUNKS // count_u, CHUNKS + (u + 1) * CHUNKS // count_u):
            far_b[c].wait_recv()
            pass_b[c].start()
        if u == begin:
            a_local.wait()
            for copy in b_local:
                copy.wait()
            for copy in near_b:
                copy.wait_recv()
            for copy in odd1:
                copy.wait_recv()
            for c in range(CHUNKS):
                pass_b[c].wait_recv()
        for g, right in enumerate((Bn0, Gn0, Bf0, Gf0)):
            if u == begin + g * count_u // 8:
                whole_group(g, right)
        if u >= lag:
            near_unit(done)
            done += 1
    for u in range(done, count_u):
        near_unit(u)
    whole_group(6, Bf1)
    for c in range(CHUNKS):
        pass_b[CHUNKS + c].wait_recv()
    whole_group(7, Gf1)

    def place(r, carry):
        rows = pl.ds(pl.multiple_of(r * size, size), size)
        for c in range(out_cols):
            out_ref[rows, c * size : (c + 1) * size] = run[ltab[r * out_cols + c]].astype(out_ref.dtype)
        return carry

    lax.fori_loop(0, half, place, 0)

    for copy in index_copies + swap + chain + chain2 + odd1 + odd3 + far_b + near_b + pass_b:
        copy.wait_send()


def local_fast(n_col, a_tiles, a_cols, a_count, b_tiles, b_cols, b_count):
    block_rows, per_row, size = a_tiles.shape[2:5]
    slots, inner = b_tiles.shape[0], b_tiles.shape[4]
    half = block_rows // 2
    terms = SHIFTS * 2 * per_row
    count = half * terms
    panels = REACH * 2
    hbm = pl.BlockSpec(memory_space=pltpu.HBM)
    vmem = pl.BlockSpec(memory_space=pltpu.VMEM)
    index_shapes = [(panels, per_row, block_rows), (panels, 1, block_rows), (4, slots, 1, inner), (4, slots, 1, inner)]
    right = pltpu.VMEM((inner, size, size), jnp.bfloat16)
    call = pl.pallas_call(
        functools.partial(gather_multiply, n_col),
        out_shape=jax.ShapeDtypeStruct((half * size, BC * size), jnp.bfloat16),
        in_specs=[hbm] * 6,
        out_specs=vmem,
        scratch_shapes=[pltpu.VMEM((REACH, 2, half, per_row, size, size), jnp.bfloat16)]
        + [right] * 8
        + [pltpu.VMEM(shape, jnp.int32) for shape in index_shapes]
        + [pltpu.SMEM(shape, jnp.int32) for shape in index_shapes]
        + [
            pltpu.VMEM((count + 1, size, size), jnp.float32),
            pltpu.SMEM((count,), jnp.int32),
            pltpu.SMEM((count,), jnp.int32),
            pltpu.SMEM((half * BC,), jnp.int32),
            pltpu.SemaphoreType.DMA((4, panels)),
            pltpu.SemaphoreType.DMA((4, panels)),
            pltpu.SemaphoreType.DMA((5, 2 * half)),
            pltpu.SemaphoreType.DMA((REACH, 2 * half)),
            pltpu.SemaphoreType.DMA((4, CHUNKS + 1)),
            pltpu.SemaphoreType.DMA((4, CHUNKS + 1)),
            pltpu.SemaphoreType.DMA((7,)),
        ],
        compiler_params=pltpu.CompilerParams(
            collective_id=0, has_side_effects=True, vmem_limit_bytes=40 * 1024 * 1024
        ),
    )
    operands = [
        jnp.swapaxes(a_cols.reshape(block_rows, per_row), 0, 1),
        a_count.reshape(1, block_rows),
        b_cols.reshape(slots, 1, inner),
        b_count.reshape(slots, 1, inner),
        a_tiles.reshape(block_rows, per_row, size, size),
        b_tiles.reshape(slots, inner, size, size),
    ]
    return call(*(pltpu.with_memory_space_constraint(x, pltpu.HBM) for x in operands))


def solution(mesh):
    placed = (
        P("row", ("col", "depth"), None, None, None, None),
        P("row", ("col", "depth"), None, None),
        P("row", ("col", "depth"), None),
        P(None, "row", "depth", "col", None, None, None, None),
        P(None, "row", "depth", "col", None, None),
        P(None, "row", "depth", "col", None),
    )
    n_col = mesh.shape["col"]
    if mesh.shape["row"] == 2 and mesh.shape["depth"] == 2 and n_col % 2 == 0 and n_col > SHIFTS:
        body = functools.partial(local_fast, n_col)
    else:
        body = local
    return jax.shard_map(
        body, mesh=mesh, in_specs=placed, out_specs=P(("row", "depth"), "col"), check_vma=False
    )
```
